32 devices in a mesh: grp: 2 (over y), seq: 4 (over z), outer: 4 (over x, core).
Axes of the slice: x: 2, y: 2, z: 4, core: 2. Of those that a mesh axis runs over, the one named last changes fastest.
Arguments:
- inputs: bfloat16 [32768, 512], P(('grp', 'outer', 'seq')), parts along dimension 0, may hold values from -6 to 6
- grad_out: bfloat16 [32768, 512], P(('grp', 'outer', 'seq')), parts along dimension 0, may hold values from -6 to 6
- w_query: bfloat16 [512, 512], replicated, may hold values from -0.25 to 0.25
- w_key: bfloat16 [512, 512], replicated, may hold values from -0.25 to 0.25
- w_value: bfloat16 [512, 512], replicated, may hold values from -0.25 to 0.25
- conv_taps: bfloat16 [4, 512], replicated, may hold values from -3 to 3
Outputs:
- grad_inputs: bfloat16 [32768, 512], P(('grp', 'outer', 'seq')), parts along dimension 0
- grad_wq: float32 [1024, 512], P('grp'), parts along dimension 0
- grad_wk: float32 [1024, 512], P('grp'), parts along dimension 0
- grad_wv: float32 [1024, 512], P('grp'), parts along dimension 0
- grad_conv: float32 [8, 512], P('grp'), parts along dimension 0
The draws below stay inside these ranges and needn't reach their ends.
There are 2 independent parts, one for each index of `grp`. The reference program is written for one: setup_inputs(seed, part) draws one part's arguments, and reference() takes and returns one part's arrays. A program takes and returns all parts, laid end to end along the dimension named above; an argument that names none is the same for every part. Nothing has to cross between parts.
All inputs are finite; a program needn't handle non-finite values.
Results may differ from the reference program's by a relative error of at most 0.0095.
Values may be sent and summed in bfloat16 or wider, within the bound.
A program may use at most 128 MiB of HBM per device.

```python
import math
import jax
import jax.numpy as jnp
from jax import lax

D = 512
HEADS = 8
HEAD_DIM = 64
TAPS = 4
BLOCK = 512
TOKENS = 16384


def levels(stream_key, dims, shards, least, top_value):
    def one(dim, blocks):
        steps = jax.random.uniform(jax.random.fold_in(jax.random.fold_in(stream_key, 6), dim), (blocks,), jnp.float32, least / len(shards), top_value / len(shards))
        return jnp.repeat(jnp.exp(steps), dims[dim] // blocks).reshape((-1,) + (1,) * (len(dims) - dim - 1))

    factor_of = one(*shards[0])
    for cut in shards[1:]:
        factor_of = factor_of * one(*cut)
    return factor_of


def normal_values(own_key, dims, scale, most, cuts=(), kind=jnp.bfloat16):
    factor_of = levels(own_key, dims, cuts, -0.22, 0.18) if cuts else 1.0
    result = jax.random.normal(own_key, dims, jnp.float32) * scale * factor_of
    return jnp.minimum(jnp.maximum(result, -most), most).astype(kind)


def setup_inputs(seed: int = 0, part: int = 0) -> dict:
    key_list = jax.random.split(jax.random.key(seed), 7)
    part_keys = jax.random.split(jax.random.fold_in(key_list[6], part), 7)
    return {
        "inputs": normal_values(part_keys[0], (TOKENS, D), 1.0, 6.0, ((0, 16),)),
        "grad_out": normal_values(part_keys[1], (TOKENS, D), 1.0, 6.0, ((0, 16),)),
        "w_query": normal_values(key_list[2], (D, D), D ** -0.5, 0.25),
        "w_key": normal_values(key_list[3], (D, D), D ** -0.5, 0.25),
        "w_value": normal_values(key_list[4], (D, D), D ** -0.5, 0.25),
        "conv_taps": normal_values(key_list[5], (TAPS, D), 0.5, 3.0),
    }


def split_heads(array, block_count):
    return array.reshape(block_count, BLOCK, HEADS, HEAD_DIM).astype(jnp.float32)

def rounded(array):
    return lax.optimization_barrier(array.astype(jnp.bfloat16)).astype(jnp.float32)

def block_grads(parts):
    queries, key_rows, value_rows, grad_rows, scales, state_prev, state_next = parts
    causal = jnp.arange(BLOCK)[:, None] >= jnp.arange(BLOCK)[None, :]
    highest = lax.Precision.HIGHEST
    scores = jnp.einsum('thj,shj->hts', grad_rows, value_rows)
    probe = rounded(jnp.where(causal[None], scores * scales[None, :, None], 0.0))
    grad_query = jnp.einsum('hts,shi->thi', probe, key_rows)
    grad_query = grad_query + scales[:, None, None] * jnp.einsum('thj,hij->thi', grad_rows, state_prev, precision=highest)
    grad_key = jnp.einsum('hts,thi->shi', probe, queries)
    grad_key = grad_key + jnp.einsum('shj,hij->shi', value_rows, state_next, precision=highest)
    affinity = jnp.einsum('thi,shi->hts', queries, key_rows)
    mixing = rounded(jnp.where(causal[None], affinity * scales[None, :, None], 0.0))
    grad_value = jnp.einsum('hts,thj->shj', mixing, grad_rows)
    grad_value = grad_value + jnp.einsum('shi,hij->shj', key_rows, state_next, precision=highest)
    return (grad_query.reshape(BLOCK, D).astype(jnp.bfloat16), grad_key.reshape(BLOCK, D).astype(jnp.bfloat16), grad_value.reshape(BLOCK, D).astype(jnp.bfloat16))

def reference(inputs, grad_out, w_query, w_key, w_value, conv_taps):
    seq_total = inputs.shape[0]
    block_count = seq_total // BLOCK
    highest = lax.Precision.HIGHEST
    queries = jnp.dot(inputs, w_query, preferred_element_type=jnp.float32).astype(jnp.bfloat16)
    keys_pre = jnp.dot(inputs, w_key, preferred_element_type=jnp.float32).astype(jnp.bfloat16)
    values = jnp.dot(inputs, w_value, preferred_element_type=jnp.float32).astype(jnp.bfloat16)
    taps = conv_taps.astype(jnp.float32)
    padded = jnp.concatenate([jnp.zeros((TAPS - 1, D), jnp.float32), keys_pre.astype(jnp.float32)], 0)
    keys = jnp.zeros((seq_total, D), jnp.float32)
    for tap_index in range(TAPS):
        keys = keys + taps[tap_index] * padded[TAPS - 1 - tap_index:TAPS - 1 - tap_index + seq_total]
    keys = keys.astype(jnp.bfloat16)
    position = jnp.arange(seq_total).astype(jnp.float32)
    scales = 1.0 / (jnp.sqrt(position + 1.0) * math.sqrt(HEAD_DIM))
    query_heads = split_heads(queries, block_count)
    key_heads = split_heads(keys, block_count)
    value_heads = split_heads(values, block_count)
    grad_heads = split_heads(grad_out, block_count)
    block_scales = scales.reshape(block_count, BLOCK)
    kv_blocks = jnp.einsum('nbhi,nbhj->nhij', key_heads, value_heads, precision=highest)
    qdo_blocks = jnp.einsum('nbhi,nbhj->nhij', query_heads * block_scales[:, :, None, None], grad_heads, precision=highest)
    state_prev = jnp.cumsum(kv_blocks, 0) - kv_blocks
    state_next = lax.optimization_barrier(jnp.sum(qdo_blocks, 0))[None] - jnp.cumsum(qdo_blocks, 0)
    grad_query, grad_key, grad_value = lax.map(block_grads, (query_heads, key_heads, value_heads, grad_heads, block_scales, state_prev, state_next))
    grad_query = grad_query.reshape(seq_total, D)
    grad_key = grad_key.reshape(seq_total, D)
    grad_value = grad_value.reshape(seq_total, D)
    key_grad32 = grad_key.astype(jnp.float32)
    after = jnp.concatenate([key_grad32, jnp.zeros((TAPS - 1, D), jnp.float32)], 0)
    grad_pre = jnp.zeros((seq_total, D), jnp.float32)
    tap_grads = []
    for tap_index in range(TAPS):
        grad_pre = grad_pre + taps[tap_index] * after[tap_index:tap_index + seq_total]
        tap_grads.append(lax.optimization_barrier(jnp.sum(key_grad32 * padded[TAPS - 1 - tap_index:TAPS - 1 - tap_index + seq_total], 0)))
    grad_pre = grad_pre.astype(jnp.bfloat16)
    grad_conv = jnp.stack(tap_grads, 0)
    grad_inputs = jnp.dot(grad_query, w_query.T, preferred_element_type=jnp.float32)
    grad_inputs = grad_inputs + jnp.dot(grad_pre, w_key.T, preferred_element_type=jnp.float32)
    grad_inputs = grad_inputs + jnp.dot(grad_value, w_value.T, preferred_element_type=jnp.float32)
    grad_wq = jnp.dot(inputs.T, grad_query, preferred_element_type=jnp.float32)
    grad_wk = jnp.dot(inputs.T, grad_pre, preferred_element_type=jnp.float32)
    grad_wv = jnp.dot(inputs.T, grad_value, preferred_element_type=jnp.float32)
    return (grad_inputs.astype(jnp.bfloat16), grad_wq, grad_wk, grad_wv, grad_conv)
```

```python
import functools
import math

import jax
import jax.numpy as jnp
from jax import lax
from jax.experimental import pallas as pl
from jax.experimental.pallas import tpu as pltpu
from jax.sharding import PartitionSpec as P

D = 512
HEADS = 8
HEAD_DIM = 64
TAPS = 4
BLOCK = 512
HALF = BLOCK // 2
TILE = 256
PAIR = 2 * HEAD_DIM
PAIRS = D // PAIR
OWNERS = 16
SLICE = PAIRS * HEAD_DIM // OWNERS
EDGE = 16
MESH = pl.DeviceIdType.MESH
BF = jnp.bfloat16
F32 = jnp.float32

NN = (((1,), (0,)), ((), ()))
NT = (((1,), (1,)), ((), ()))
TN = (((0,), (0,)), ((), ()))


def mm(a, b, dims):
    return lax.dot_general(a, b, dims, preferred_element_type=F32)


def kernel(
    seq_count, outer_count,
    inp, go, wq, wk, wv, taps_ref,
    gin, out, conv_out,
    kp32, q, qs, k, v, gs, xt, gva, gq, gk32, gv, gp,
    edge_k, edge_kr, edge_g, edge_gr,
    kvb, qdb, sb, rb, so, st, sp, sn,
    wb, rc, sx, rx, sz, rz, cown, crecv,
    edge_sem, s1_send, s1_recv, s2_send, s2_recv, cv_send, cv_recv,
    c_sem, x_send, x_recv, z_send, z_recv, az_send, az_recv, ax_send, ax_recv, ac_sem,
):
    Z = seq_count
    X = outer_count // 2
    N = seq_count * outer_count
    length = inp.shape[0]
    blocks = length // BLOCK
    tiles = length // TILE
    steps = blocks * PAIRS
    r = D // N
    z = lax.axis_index("seq")
    o = lax.axis_index("outer")
    x, core = o // 2, o % 2
    me = o * Z + z

    def at(place):
        return {"seq": place % Z, "outer": place // Z}

    def others(count, mine, body):
        def one(i, carry):
            @pl.when(i != mine)
            def _():
                body(i)
            return carry
        lax.fori_loop(0, count, one, 0)

    def remote(src, dst, send, recv, device):
        return pltpu.make_async_remote_copy(
            src_ref=src, dst_ref=dst, send_sem=send, recv_sem=recv,
            device_id=device, device_id_type=MESH,
        )

    barrier = pltpu.get_barrier_semaphore()
    others(N, me, lambda i: pl.semaphore_signal(
        barrier, inc=1, device_id=at(i), device_id_type=MESH))

    lane = lax.broadcasted_iota(jnp.int32, (1, PAIR), 1)
    low = jnp.where(lane < HEAD_DIM, 1.0, 0.0)
    high = 1.0 - low
    masks = (low.astype(BF), high.astype(BF))

    def keys_tile(i, carry):
        rows = pl.ds(pl.multiple_of(i * TILE, TILE), TILE)
        res = mm(inp[rows, :], wk[...], NN).astype(BF).astype(F32)
        kp32[pl.ds(pl.multiple_of(i * TILE + 8, 8), TILE), :] = res
        return carry

    lax.fori_loop(0, tiles, keys_tile, 0)
    edge_k[...] = kp32[8 + length - EDGE : 8 + length, :].astype(BF)

    pl.semaphore_wait(barrier, N - 1)
    after, ahead = (me + 1) % N, (me + N - 1) % N
    send_k = remote(edge_k, edge_kr, edge_sem.at[0], edge_sem.at[1], at(after))
    send_k.start()

    def rest_tile(i, carry):
        start = pl.multiple_of(i * TILE, TILE)
        rows = pl.ds(start, TILE)
        place = lax.broadcasted_iota(jnp.int32, (TILE, 128), 0) + (me * length + start)
        scale = 1.0 / (jnp.sqrt(place.astype(F32) + 1.0) * math.sqrt(HEAD_DIM))
        scale = jnp.concatenate([scale] * (D // 128), 1)
        block = inp[rows, :]
        queries = mm(block, wq[...], NN).astype(BF)
        q[rows, :] = queries
        qs[rows, :] = (queries.astype(F32) * scale).astype(BF)
        v[rows, :] = mm(block, wv[...], NN).astype(BF)
        gs[rows, :] = (go[rows, :].astype(F32) * scale).astype(BF)
        xt[:, rows] = block.T
        return carry

    lax.fori_loop(0, tiles, rest_tile, 0)
    taps = taps_ref[...].astype(F32)
    send_k.wait()
    keep = jnp.where(me == 0, 0.0, 1.0)
    kp32[0:8, :] = edge_kr[EDGE - 8 : EDGE, :].astype(F32) * keep

    def conv_tile(i, carry):
        start = pl.multiple_of(i * TILE, TILE)
        rows = kp32[pl.ds(start, TILE + 8), :]
        total = taps[0:1] * rows[8 : 8 + TILE]
        for j in range(1, TAPS):
            total = total + taps[j : j + 1] * rows[8 - j : 8 - j + TILE]
        k[pl.ds(start, TILE), :] = total.astype(BF)
        return carry

    lax.fori_loop(0, tiles, conv_tile, 0)

    def shrink(full):
        return full[:HEAD_DIM] * low + full[HEAD_DIM:] * high

    for p in range(PAIRS):
        cols = slice(p * PAIR, (p + 1) * PAIR)
        kv_sum = qd_sum = None
        for b in range(blocks):
            rows = slice(b * BLOCK, (b + 1) * BLOCK)
            kv = shrink(mm(k[rows, cols], v[rows, cols], TN))
            qd = shrink(mm(qs[rows, cols], go[rows, cols], TN))
            kvb[b, p] = kv
            qdb[b, p] = qd
            kv_sum = kv if kv_sum is None else kv_sum + kv
            qd_sum = qd if qd_sum is None else qd_sum + qd
        per = HEAD_DIM // SLICE
        for u in range(per):
            sb[p * per + u, 0] = kv_sum[u * SLICE : (u + 1) * SLICE].astype(BF)
            sb[p * per + u, 1] = qd_sum[u * SLICE : (u + 1) * SLICE].astype(BF)

    def to_owner(i):
        return remote(sb.at[i], rb.at[me], s1_send.at[i], s1_recv.at[me], at(i))

    def from_member(i):
        return remote(sb.at[0], rb.at[i], s1_send.at[0], s1_recv.at[i], at(i))

    def to_member(i):
        return remote(so.at[i], st.at[me], s2_send.at[i], s2_recv.at[me], at(i))

    def from_owner(i):
        return remote(so.at[0], st.at[i], s2_send.at[0], s2_recv.at[i], at(i))

    def as_owner(body):
        if N > OWNERS:
            pl.when(me < OWNERS)(body)
        else:
            body()

    others(OWNERS, me, lambda i: to_owner(i).start())

    def attend(first, second, third, keys_first, index):
        b, p = index // PAIRS, index % PAIRS
        lanes = pl.ds(pl.multiple_of(p * PAIR, PAIR), PAIR)
        base = b * BLOCK
        lo = pl.ds(pl.multiple_of(base, HALF), HALF)
        hi = pl.ds(pl.multiple_of(base + HALF, HALF), HALF)
        row = lax.broadcasted_iota(jnp.int32, (HALF, HALF), 0)
        col = lax.broadcasted_iota(jnp.int32, (HALF, HALF), 1)
        causal = row <= col if keys_first else row >= col
        a_lo, a_hi = first[lo, lanes], first[hi, lanes]
        b_lo, b_hi = second[lo, lanes], second[hi, lanes]
        c_lo, c_hi = third[lo, lanes], third[hi, lanes]
        res_lo = res_hi = None
        for mask in masks:
            al, ah = a_lo * mask, a_hi * mask
            cl, ch = c_lo * mask, c_hi * mask
            s_ll = jnp.where(causal, mm(al, b_lo, NT), 0.0).astype(BF)
            s_hh = jnp.where(causal, mm(ah, b_hi, NT), 0.0).astype(BF)
            if keys_first:
                s_x = mm(al, b_hi, NT).astype(BF)
                one_lo = mm(s_ll, cl, NN) + mm(s_x, ch, NN)
                one_hi = mm(s_hh, ch, NN)
            else:
                s_x = mm(ah, b_lo, NT).astype(BF)
                one_lo = mm(s_ll, cl, NN)
                one_hi = mm(s_hh, ch, NN) + mm(s_x, cl, NN)
            res_lo = one_lo if res_lo is None else res_lo + one_lo
            res_hi = one_hi if res_hi is None else res_hi + one_hi
        return b, p, lanes, lo, hi, res_lo, res_hi

    def value_step(index, carry):
        _, _, lanes, lo, hi, res_lo, res_hi = attend(k, qs, go, True, index)
        gva[lo, lanes] = res_lo
        gva[hi, lanes] = res_hi
        return carry

    half = PAIRS * (blocks // 2)
    lax.fori_loop(0, half, value_step, 0)

    @as_owner
    def _():
        others(N, me, lambda i: from_member(i).wait_recv())
        rb[me] = sb[me]

        def prefix(i, carry):
            so[i, 0] = carry.astype(BF)
            return carry + rb[i, 0].astype(F32)

        lax.fori_loop(0, N, prefix, jnp.zeros((SLICE, PAIR), F32))

        def suffix(i, carry):
            so[N - 1 - i, 1] = carry.astype(BF)
            return carry + rb[N - 1 - i, 1].astype(F32)

        lax.fori_loop(0, N, suffix, jnp.zeros((SLICE, PAIR), F32))
        st[me] = so[me]
        others(N, me, lambda i: to_member(i).start())

    lax.fori_loop(half, steps, value_step, 0)
    others(OWNERS, me, lambda i: from_owner(i).wait_recv())

    per = HEAD_DIM // SLICE
    for p in range(PAIRS):
        prev = st[p * per : (p + 1) * per, 0].astype(F32).reshape(HEAD_DIM, PAIR)
        for b in range(blocks):
            sp[b, p] = jnp.concatenate([prev * low, prev * high], 0).astype(BF)
            prev = prev + kvb[b, p]
        later = st[p * per : (p + 1) * per, 1].astype(F32).reshape(HEAD_DIM, PAIR)
        for b in reversed(range(blocks)):
            sn[b, p] = jnp.concatenate([later * low, later * high], 0).astype(BF)
            later = later + qdb[b, p]

    def value_finish(index, carry):
        b, p = index // PAIRS, index % PAIRS
        lanes = pl.ds(pl.multiple_of(p * PAIR, PAIR), PAIR)
        rows = pl.ds(pl.multiple_of(b * BLOCK, BLOCK), BLOCK)
        gv[rows, lanes] = (gva[rows, lanes] + mm(k[rows, lanes], sn[b, p], NN)).astype(BF)
        return carry

    lax.fori_loop(0, steps, value_finish, 0)

    def weight(c, grads):
        for h in range(2):
            res = mm(xt[h * HALF : (h + 1) * HALF, :], grads[...], NN).astype(BF)
            for i in range(X * Z):
                wb[c, h, i // Z, i % Z] = res[r * i : r * i + r]

    def core_copy(c):
        return remote(wb.at[c, 1 - core], rc.at[c], c_sem.at[c, 0], c_sem.at[c, 1],
                      {"outer": x * 2 + 1 - core})

    def x_copy(c, i, source):
        return remote(sx.at[c, i], rx.at[c, source], x_send.at[c, i], x_recv.at[c, source],
                      {"outer": i * 2 + core})

    def z_copy(c, i, source):
        return remote(sz.at[c, i], rz.at[c, source], z_send.at[c, i], z_recv.at[c, source],
                      {"seq": i})

    def az_copy(c, i, source):
        slot = out.at[c, core, x, source]
        return remote(slot, slot, az_send.at[c, i], az_recv.at[c, source], {"seq": i})

    def ax_copy(c, i, source):
        slot = out.at[c, core, source]
        return remote(slot, slot, ax_send.at[c, i], ax_recv.at[c, source],
                      {"outer": i * 2 + core})

    def ac_copy(c, source):
        slot = out.at[c, source]
        return remote(slot, slot, ac_sem.at[c, 0], ac_sem.at[c, 1],
                      {"outer": x * 2 + 1 - core})

    def stage_core(c):
        core_copy(c).start()

    def stage_x(c):
        core_copy(c).wait_recv()
        for i in range(X):
            sx[c, i] = (wb[c, core, i].astype(F32) + rc[c, i].astype(F32)).astype(BF)
        others(X, x, lambda i: x_copy(c, i, x).start())

    def stage_z(c):
        others(X, x, lambda i: x_copy(c, i, i).wait_recv())
        rx[c, x] = sx[c, x]
        total = rx[c, 0].astype(F32)
        for i in range(1, X):
            total = total + rx[c, i].astype(F32)
        sz[c] = total.astype(BF)
        others(Z, z, lambda i: z_copy(c, i, z).start())

    def stage_az(c):
        others(Z, z, lambda i: z_copy(c, i, i).wait_recv())
        rz[c, z] = sz[c, z]
        total = rz[c, 0].astype(F32)
        for i in range(1, Z):
            total = total + rz[c, i].astype(F32)
        out[c, core, x, z] = total.astype(BF)
        others(Z, z, lambda i: az_copy(c, i, z).start())

    def stage_ax(c):
        others(Z, z, lambda i: az_copy(c, i, i).wait_recv())
        others(X, x, lambda i: ax_copy(c, i, x).start())

    def stage_ac(c):
        others(X, x, lambda i: ax_copy(c, i, i).wait_recv())
        ac_copy(c, core).start()

    def stage_end(c):
        ac_copy(c, 1 - core).wait_recv()
        core_copy(c).wait_send()
        others(X, x, lambda i: x_copy(c, i, x).wait_send())
        others(Z, z, lambda i: z_copy(c, i, z).wait_send())
        others(Z, z, lambda i: az_copy(c, i, z).wait_send())
        others(X, x, lambda i: ax_copy(c, i, x).wait_send())
        ac_copy(c, core).wait_send()

    weight(0, gv)
    stage_core(0)

    def query_step(index, carry):
        b, p, lanes, lo, hi, res_lo, res_hi = attend(gs, v, k, False, index)
        state = sp[b, p]
        gq[lo, lanes] = (res_lo + mm(gs[lo, lanes], state, NT)).astype(BF)
        gq[hi, lanes] = (res_hi + mm(gs[hi, lanes], state, NT)).astype(BF)
        return carry

    lax.fori_loop(0, half, query_step, 0)
    stage_x(0)
    lax.fori_loop(half, steps, query_step, 0)
    weight(1, gq)
    stage_core(1)
    stage_z(0)

    def key_step(index, carry):
        b, p, lanes, lo, hi, res_lo, res_hi = attend(v, gs, q, True, index)
        state = sn[b, p]
        gk32[lo, lanes] = (res_lo + mm(v[lo, lanes], state, NT)).astype(BF).astype(F32)
        gk32[hi, lanes] = (res_hi + mm(v[hi, lanes], state, NT)).astype(BF).astype(F32)
        return carry

    lax.fori_loop(0, half, key_step, 0)
    edge_g[...] = gk32[0:EDGE, :].astype(BF)
    send_g = remote(edge_g, edge_gr, edge_sem.at[2], edge_sem.at[3], at(ahead))
    send_g.start()
    stage_x(1)
    stage_az(0)
    lax.fori_loop(half, steps, key_step, 0)
    stage_z(1)
    stage_ax(0)

    send_g.wait()
    keep_g = jnp.where(me == N - 1, 0.0, 1.0)
    gk32[length : length + 8, :] = edge_gr[0:8, :].astype(F32) * keep_g

    def pre_tile(i, sums):
        start = pl.multiple_of(i * TILE, TILE)
        rows = gk32[pl.ds(start, TILE + 8), :]
        keys = kp32[pl.ds(start, TILE + 8), :]
        own = rows[0:TILE]
        total = taps[0:1] * own
        for j in range(1, TAPS):
            total = total + taps[j : j + 1] * rows[j : j + TILE]
        gp[pl.ds(start, TILE), :] = total.astype(BF)
        return tuple(
            sums[j] + jnp.sum((own * keys[8 - j : 8 - j + TILE]).reshape(TILE // 8, 8, D), 0)
            for j in range(TAPS)
        )

    sums = lax.fori_loop(0, tiles, pre_tile, tuple(jnp.zeros((8, D), F32) for _ in range(TAPS)))
    for j in range(TAPS):
        cown[j : j + 1, :] = jnp.sum(sums[j], 0, keepdims=True)

    def conv_copy(i, source):
        return remote(cown, crecv.at[source], cv_send.at[i], cv_recv.at[source], at(i))

    weight(2, gp)
    stage_core(2)
    stage_ac(0)
    stage_az(1)
    others(N, me, lambda i: conv_copy(i, me).start())

    def gin_tile(i, carry):
        rows = pl.ds(pl.multiple_of(i * TILE, TILE), TILE)
        total = mm(gq[rows, :], wq[...], NT)
        total = total + mm(gp[rows, :], wk[...], NT)
        total = total + mm(gv[rows, :], wv[...], NT)
        gin[rows, :] = total.astype(BF)
        return carry

    stage_x(2)
    lax.fori_loop(0, tiles // 2, gin_tile, 0)
    stage_ax(1)
    stage_z(2)
    lax.fori_loop(tiles // 2, tiles, gin_tile, 0)
    stage_ac(1)
    stage_az(2)
    others(N, me, lambda i: conv_copy(i, i).wait_recv())
    crecv[me] = cown[...]
    conv_out[...] = lax.fori_loop(
        1, N, lambda i, total: total + crecv[i], crecv[0])
    stage_ax(2)
    stage_ac(2)
    others(OWNERS, me, lambda i: to_owner(i).wait_send())

    @as_owner
    def _():
        others(N, me, lambda i: to_member(i).wait_send())

    others(N, me, lambda i: conv_copy(i, me).wait_send())
    stage_end(0)
    stage_end(1)
    stage_end(2)


def on_device(seq_count, outer_count, inputs, grad_out, w_query, w_key, w_value, conv_taps):
    length = inputs.shape[0]
    Z, X = seq_count, outer_count // 2
    N = seq_count * outer_count
    r = D // N
    blocks = length // BLOCK
    vm = pltpu.VMEM
    dma = pltpu.SemaphoreType.DMA
    full = vm((length, D), BF)
    edge = vm((EDGE, D), BF)
    state = vm((blocks, PAIRS, HEAD_DIM, PAIR), F32)
    member = vm((N, 2, SLICE, PAIR), BF)
    owner = vm((OWNERS, 2, SLICE, PAIR), BF)
    square = vm((blocks, PAIRS, PAIR, PAIR), BF)
    scratch = [
        vm((length + 8, D), F32), full, full, full, full, full, vm((D, length), BF),
        vm((length, D), F32), full, vm((length + 8, D), F32), full, full,
        edge, edge, edge, edge,
        state, state, owner, member, member, owner, square, square,
        vm((3, 2, X, Z, r, D), BF), vm((3, X, Z, r, D), BF), vm((3, X, Z, r, D), BF),
        vm((3, X, Z, r, D), BF), vm((3, Z, r, D), BF), vm((3, Z, r, D), BF),
        vm((TAPS, D), F32), vm((N, TAPS, D), F32),
        dma((4,)), dma((OWNERS,)), dma((N,)), dma((N,)), dma((OWNERS,)), dma((N,)), dma((N,)),
        dma((3, 2)), dma((3, X)), dma((3, X)), dma((3, Z)), dma((3, Z)),
        dma((3, Z)), dma((3, Z)), dma((3, X)), dma((3, X)), dma((3, 2)),
    ]
    spec = pl.BlockSpec(memory_space=pltpu.VMEM)
    grad_inputs, weights, grad_conv = pl.pallas_call(
        functools.partial(kernel, seq_count, outer_count),
        out_shape=(
            jax.ShapeDtypeStruct((length, D), BF),
            jax.ShapeDtypeStruct((3, 2, X, Z, r, D), BF),
            jax.ShapeDtypeStruct((TAPS, D), F32),
        ),
        in_specs=[spec] * 6,
        out_specs=(spec, spec, spec),
        scratch_shapes=scratch,
        compiler_params=pltpu.CompilerParams(
            collective_id=0, has_side_effects=True, vmem_limit_bytes=56 * 1024 * 1024
        ),
    )(inputs, grad_out, w_query, w_key, w_value, conv_taps)
    weights = weights.reshape(3, D, D).astype(F32)
    return (grad_inputs, weights[1], weights[2], weights[0], grad_conv)


def solution(mesh):
    rows = P(("grp", "outer", "seq"), None)
    body = functools.partial(on_device, mesh.shape["seq"], mesh.shape["outer"])
    return jax.shard_map(
        body,
        mesh=mesh,
        in_specs=(rows, rows, P(), P(), P(), P()),
        out_specs=(rows, P("grp", None), P("grp", None), P("grp", None), P("grp", None)),
        check_vma=False,
    )
```

```python
import functools
import math

import jax
import jax.numpy as jnp
from jax import lax
from jax.experimental import pallas as pl
from jax.experimental.pallas import tpu as pltpu
from jax.sharding import PartitionSpec as P

D = 512
HEADS = 8
HEAD_DIM = 64
TAPS = 4
BLOCK = 512
HALF = BLOCK // 2
TILE = 256
PAIR = 2 * HEAD_DIM
PAIRS = D // PAIR
EDGE = 16
MESH = pl.DeviceIdType.MESH
BF = jnp.bfloat16
F32 = jnp.float32

NN = (((1,), (0,)), ((), ()))
NT = (((1,), (1,)), ((), ()))
TN = (((0,), (0,)), ((), ()))


def mm(a, b, dims):
    return lax.dot_general(a, b, dims, preferred_element_type=F32)


def kernel(
    seq_count, outer_count,
    inp, go, wq, wk, wv, taps_ref,
    gin, out, conv_out,
    kp32, q, qs, k, v, gs, xt, gva, gqa, gq, gk32, gv, gp,
    edge_k, edge_kr, edge_g, edge_gr,
    kvb, qdb, sb, rb, part, tot, trecv, so, st, sp, sn,
    wb, rc, sx, rx, sz, rz, csend, crc, crx, crz,
    edge_sem, s1_send, s1_recv, t_send, t_recv, s2_send, s2_recv, cv_c, cv_x, cv_z,
    c_sem, x_send, x_recv, z_send, z_recv, az_send, az_recv, ax_send, ax_recv, ac_sem,
):
    Z = seq_count
    X = outer_count // 2
    N = seq_count * outer_count
    length = inp.shape[0]
    blocks = length // BLOCK
    tiles = length // TILE
    steps = blocks * PAIRS
    r = D // N
    rows_z = PAIRS * HEAD_DIM // Z
    z = lax.axis_index("seq")
    o = lax.axis_index("outer")
    x, core = o // 2, o % 2
    me = o * Z + z

    def at(place):
        return {"seq": place % Z, "outer": place // Z}

    def others(count, mine, body):
        def one(i, carry):
            @pl.when(i != mine)
            def _():
                body(i)
            return carry
        lax.fori_loop(0, count, one, 0)

    def remote(src, dst, send, recv, device):
        return pltpu.make_async_remote_copy(
            src_ref=src, dst_ref=dst, send_sem=send, recv_sem=recv,
            device_id=device, device_id_type=MESH,
        )

    barrier = pltpu.get_barrier_semaphore()
    after, ahead = (me + 1) % N, (me + N - 1) % N

    def greet(device):
        pl.semaphore_signal(barrier, inc=1, device_id=device, device_id_type=MESH)

    others(Z, z, lambda i: greet({"seq": i}))
    others(outer_count, o, lambda i: greet({"outer": i}))
    greet(at(after))
    greet(at(ahead))

    lane = lax.broadcasted_iota(jnp.int32, (1, PAIR), 1)
    low = jnp.where(lane < HEAD_DIM, 1.0, 0.0)
    high = 1.0 - low
    masks = (low.astype(BF), high.astype(BF))

    def keys_tile(i, carry):
        rows = pl.ds(pl.multiple_of(i * TILE, TILE), TILE)
        res = mm(inp[rows, :], wk[...], NN).astype(BF).astype(F32)
        kp32[pl.ds(pl.multiple_of(i * TILE + 8, 8), TILE), :] = res
        return carry

    lax.fori_loop(0, tiles, keys_tile, 0)
    edge_k[...] = kp32[8 + length - EDGE : 8 + length, :].astype(BF)

    pl.semaphore_wait(barrier, Z + outer_count)
    send_k = remote(edge_k, edge_kr, edge_sem.at[0], edge_sem.at[1], at(after))
    send_k.start()

    def rest_tile(i, carry):
        start = pl.multiple_of(i * TILE, TILE)
        rows = pl.ds(start, TILE)
        place = lax.broadcasted_iota(jnp.int32, (TILE, 128), 0) + (me * length + start)
        scale = 1.0 / (jnp.sqrt(place.astype(F32) + 1.0) * math.sqrt(HEAD_DIM))
        scale = jnp.concatenate([scale] * (D // 128), 1)
        block = inp[rows, :]
        queries = mm(block, wq[...], NN).astype(BF)
        q[rows, :] = queries
        qs[rows, :] = (queries.astype(F32) * scale).astype(BF)
        v[rows, :] = mm(block, wv[...], NN).astype(BF)
        gs[rows, :] = (go[rows, :].astype(F32) * scale).astype(BF)
        return carry

    lax.fori_loop(0, tiles, rest_tile, 0)
    taps = taps_ref[...].astype(F32)
    send_k.wait()
    keep = jnp.where(me == 0, 0.0, 1.0)
    kp32[0:8, :] = edge_kr[EDGE - 8 : EDGE, :].astype(F32) * keep

    def conv_tile(i, carry):
        start = pl.multiple_of(i * TILE, TILE)
        rows = kp32[pl.ds(start, TILE + 8), :]
        total = taps[0:1] * rows[8 : 8 + TILE]
        for j in range(1, TAPS):
            total = total + taps[j : j + 1] * rows[8 - j : 8 - j + TILE]
        k[pl.ds(start, TILE), :] = total.astype(BF)
        return carry

    lax.fori_loop(0, tiles, conv_tile, 0)

    def shrink(full):
        return full[:HEAD_DIM] * low + full[HEAD_DIM:] * high

    for p in range(PAIRS):
        cols = slice(p * PAIR, (p + 1) * PAIR)
        kv_sum = qd_sum = None
        for b in range(blocks):
            rows = slice(b * BLOCK, (b + 1) * BLOCK)
            kv = shrink(mm(k[rows, cols], v[rows, cols], TN))
            qd = shrink(mm(qs[rows, cols], go[rows, cols], TN))
            kvb[b, p] = kv
            qdb[b, p] = qd
            kv_sum = kv if kv_sum is None else kv_sum + kv
            qd_sum = qd if qd_sum is None else qd_sum + qd
        per = HEAD_DIM // rows_z
        for u in range(per):
            cut = slice(u * rows_z, (u + 1) * rows_z)
            sb[p * per + u, 0] = kv_sum[cut].astype(BF)
            sb[p * per + u, 1] = qd_sum[cut].astype(BF)

    def to_owner(i, source):
        return remote(sb.at[i], rb.at[source], s1_send.at[i], s1_recv.at[source], {"seq": i})

    def to_outer(i, source):
        return remote(tot, trecv.at[source], t_send.at[i], t_recv.at[source], {"outer": i})

    def to_member(i, source):
        return remote(so.at[i], st.at[source], s2_send.at[i], s2_recv.at[source], {"seq": i})

    others(Z, z, lambda i: to_owner(i, z).start())

    def attend(first, second, third, keys_first, index):
        b, p = index // PAIRS, index % PAIRS
        lanes = pl.ds(pl.multiple_of(p * PAIR, PAIR), PAIR)
        base = b * BLOCK
        lo = pl.ds(pl.multiple_of(base, HALF), HALF)
        hi = pl.ds(pl.multiple_of(base + HALF, HALF), HALF)
        row = lax.broadcasted_iota(jnp.int32, (HALF, HALF), 0)
        col = lax.broadcasted_iota(jnp.int32, (HALF, HALF), 1)
        causal = row <= col if keys_first else row >= col
        a_lo, a_hi = first[lo, lanes], first[hi, lanes]
        b_lo, b_hi = second[lo, lanes], second[hi, lanes]
        c_lo, c_hi = third[lo, lanes], third[hi, lanes]
        res_lo = res_hi = None
        for mask in masks:
            al, ah = a_lo * mask, a_hi * mask
            cl, ch = c_lo * mask, c_hi * mask
            s_ll = jnp.where(causal, mm(al, b_lo, NT), 0.0).astype(BF)
            s_hh = jnp.where(causal, mm(ah, b_hi, NT), 0.0).astype(BF)
            if keys_first:
                s_x = mm(al, b_hi, NT).astype(BF)
                one_lo = mm(s_ll, cl, NN) + mm(s_x, ch, NN)
                one_hi = mm(s_hh, ch, NN)
            else:
                s_x = mm(ah, b_lo, NT).astype(BF)
                one_lo = mm(s_ll, cl, NN)
                one_hi = mm(s_hh, ch, NN) + mm(s_x, cl, NN)
            res_lo = one_lo if res_lo is None else res_lo + one_lo
            res_hi = one_hi if res_hi is None else res_hi + one_hi
        return b, p, lanes, lo, hi, res_lo, res_hi

    def value_step(index, carry):
        _, _, lanes, lo, hi, res_lo, res_hi = attend(k, qs, go, True, index)
        gva[lo, lanes] = res_lo
        gva[hi, lanes] = res_hi
        return carry

    half = PAIRS * (blocks // 2)
    lax.fori_loop(0, half, value_step, 0)

    others(Z, z, lambda i: to_owner(i, i).wait_recv())
    rb[z] = sb[z]
    total = jnp.zeros((rows_z, PAIR), F32)
    for i in range(Z):
        part[i, 0] = total
        total = total + rb[i, 0].astype(F32)
    tot[0] = total.astype(BF)
    total = jnp.zeros((rows_z, PAIR), F32)
    for i in reversed(range(Z)):
        part[i, 1] = total
        total = total + rb[i, 1].astype(F32)
    tot[1] = total.astype(BF)
    others(outer_count, o, lambda i: to_outer(i, o).start())
    lax.fori_loop(half, steps, value_step, 0)
    others(outer_count, o, lambda i: to_outer(i, i).wait_recv())
    trecv[o] = tot[...]
    earlier = jnp.zeros((rows_z, PAIR), F32)
    later = jnp.zeros((rows_z, PAIR), F32)
    for i in range(outer_count):
        earlier = earlier + trecv[i, 0].astype(F32) * jnp.where(i < o, 1.0, 0.0)
        later = later + trecv[i, 1].astype(F32) * jnp.where(i > o, 1.0, 0.0)
    for i in range(Z):
        so[i, 0] = (earlier + part[i, 0]).astype(BF)
        so[i, 1] = (later + part[i, 1]).astype(BF)
    st[z] = so[z]
    others(Z, z, lambda i: to_member(i, z).start())

    def query_early(index, carry):
        _, _, lanes, lo, hi, res_lo, res_hi = attend(gs, v, k, False, index)
        gqa[lo, lanes] = res_lo
        gqa[hi, lanes] = res_hi
        return carry

    lax.fori_loop(0, half, query_early, 0)
    for i in range(tiles):
        xt[:, i * TILE : (i + 1) * TILE] = inp[i * TILE : (i + 1) * TILE, :].T
    others(Z, z, lambda i: to_member(i, i).wait_recv())

    per = HEAD_DIM // rows_z
    for p in range(PAIRS):
        prev = st[p * per : (p + 1) * per, 0].astype(F32).reshape(HEAD_DIM, PAIR)
        for b in range(blocks):
            sp[b, p] = jnp.concatenate([prev * low, prev * high], 0).astype(BF)
            prev = prev + kvb[b, p]
        later = st[p * per : (p + 1) * per, 1].astype(F32).reshape(HEAD_DIM, PAIR)
        for b in reversed(range(blocks)):
            sn[b, p] = jnp.concatenate([later * low, later * high], 0).astype(BF)
            later = later + qdb[b, p]

    def value_finish(index, carry):
        b, p = index // PAIRS, index % PAIRS
        lanes = pl.ds(pl.multiple_of(p * PAIR, PAIR), PAIR)
        rows = pl.ds(pl.multiple_of(b * BLOCK, BLOCK), BLOCK)
        gv[rows, lanes] = (gva[rows, lanes] + mm(k[rows, lanes], sn[b, p], NN)).astype(BF)
        return carry

    lax.fori_loop(0, steps, value_finish, 0)

    def weight(c, grads):
        for h in range(2):
            res = mm(xt[h * HALF : (h + 1) * HALF, :], grads[...], NN).astype(BF)
            for i in range(X * Z):
                wb[c, h, i // Z, i % Z] = res[r * i : r * i + r]

    def core_copy(c):
        return remote(wb.at[c, 1 - core], rc.at[c], c_sem.at[c, 0], c_sem.at[c, 1],
                      {"outer": x * 2 + 1 - core})

    def x_copy(c, i, source):
        return remote(sx.at[c, i], rx.at[c, source], x_send.at[c, i], x_recv.at[c, source],
                      {"outer": i * 2 + core})

    def z_copy(c, i, source):
        return remote(sz.at[c, i], rz.at[c, source], z_send.at[c, i], z_recv.at[c, source],
                      {"seq": i})

    def az_copy(c, i, source):
        slot = out.at[c, core, x, source]
        return remote(slot, slot, az_send.at[c, i], az_recv.at[c, source], {"seq": i})

    def ax_copy(c, i, source):
        slot = out.at[c, core, source]
        return remote(slot, slot, ax_send.at[c, i], ax_recv.at[c, source],
                      {"outer": i * 2 + core})

    def ac_copy(c, source):
        slot = out.at[c, source]
        return remote(slot, slot, ac_sem.at[c, 0], ac_sem.at[c, 1],
                      {"outer": x * 2 + 1 - core})

    def stage_core(c):
        core_copy(c).start()

    def stage_x(c):
        core_copy(c).wait_recv()
        for i in range(X):
            sx[c, i] = (wb[c, core, i].astype(F32) + rc[c, i].astype(F32)).astype(BF)
        others(X, x, lambda i: x_copy(c, i, x).start())

    def stage_z(c):
        others(X, x, lambda i: x_copy(c, i, i).wait_recv())
        rx[c, x] = sx[c, x]
        total = rx[c, 0].astype(F32)
        for i in range(1, X):
            total = total + rx[c, i].astype(F32)
        sz[c] = total.astype(BF)
        others(Z, z, lambda i: z_copy(c, i, z).start())

    def stage_az(c):
        others(Z, z, lambda i: z_copy(c, i, i).wait_recv())
        rz[c, z] = sz[c, z]
        total = rz[c, 0].astype(F32)
        for i in range(1, Z):
            total = total + rz[c, i].astype(F32)
        out[c, core, x, z] = total.astype(BF)
        others(Z, z, lambda i: az_copy(c, i, z).start())

    def stage_ax(c):
        others(Z, z, lambda i: az_copy(c, i, i).wait_recv())
        others(X, x, lambda i: ax_copy(c, i, x).start())

    def stage_ac(c):
        others(X, x, lambda i: ax_copy(c, i, i).wait_recv())
        ac_copy(c, core).start()

    def stage_end(c):
        ac_copy(c, 1 - core).wait_recv()
        core_copy(c).wait_send()
        others(X, x, lambda i: x_copy(c, i, x).wait_send())
        others(Z, z, lambda i: z_copy(c, i, z).wait_send())
        others(Z, z, lambda i: az_copy(c, i, z).wait_send())
        others(X, x, lambda i: ax_copy(c, i, x).wait_send())
        ac_copy(c, core).wait_send()

    weight(0, gv)
    stage_core(0)

    def query_step(index, carry):
        b, p, lanes, lo, hi, res_lo, res_hi = attend(gs, v, k, False, index)
        state = sp[b, p]
        gq[lo, lanes] = (res_lo + mm(gs[lo, lanes], state, NT)).astype(BF)
        gq[hi, lanes] = (res_hi + mm(gs[hi, lanes], state, NT)).astype(BF)
        return carry

    def query_finish(index, carry):
        b, p = index // PAIRS, index % PAIRS
        lanes = pl.ds(pl.multiple_of(p * PAIR, PAIR), PAIR)
        rows = pl.ds(pl.multiple_of(b * BLOCK, BLOCK), BLOCK)
        gq[rows, lanes] = (gqa[rows, lanes] + mm(gs[rows, lanes], sp[b, p], NT)).astype(BF)
        return carry

    lax.fori_loop(0, half, query_finish, 0)
    lax.fori_loop(half, steps, query_step, 0)
    stage_x(0)
    weight(1, gq)
    stage_core(1)

    def key_step(index, carry):
        b, p, lanes, lo, hi, res_lo, res_hi = attend(v, gs, q, True, index)
        state = sn[b, p]
        gk32[lo, lanes] = (res_lo + mm(v[lo, lanes], state, NT)).astype(BF).astype(F32)
        gk32[hi, lanes] = (res_hi + mm(v[hi, lanes], state, NT)).astype(BF).astype(F32)
        return carry

    lax.fori_loop(0, half, key_step, 0)
    edge_g[...] = gk32[0:EDGE, :].astype(BF)
    send_g = remote(edge_g, edge_gr, edge_sem.at[2], edge_sem.at[3], at(ahead))
    send_g.start()
    stage_x(1)
    stage_z(0)
    lax.fori_loop(half, steps, key_step, 0)

    send_g.wait()
    keep_g = jnp.where(me == N - 1, 0.0, 1.0)
    gk32[length : length + 8, :] = edge_gr[0:8, :].astype(F32) * keep_g

    def pre_tile(i, sums):
        start = pl.multiple_of(i * TILE, TILE)
        rows = gk32[pl.ds(start, TILE + 8), :]
        keys = kp32[pl.ds(start, TILE + 8), :]
        own = rows[0:TILE]
        total = taps[0:1] * own
        for j in range(1, TAPS):
            total = total + taps[j : j + 1] * rows[j : j + TILE]
        gp[pl.ds(start, TILE), :] = total.astype(BF)
        return tuple(
            sums[j] + jnp.sum((own * keys[8 - j : 8 - j + TILE]).reshape(TILE // 8, 8, D), 0)
            for j in range(TAPS)
        )

    sums = lax.fori_loop(0, tiles, pre_tile, tuple(jnp.zeros((8, D), F32) for _ in range(TAPS)))
    for j in range(TAPS):
        csend[0, j : j + 1, :] = jnp.sum(sums[j], 0, keepdims=True)

    conv_core = remote(csend.at[0], crc, cv_c.at[0], cv_c.at[1], {"outer": x * 2 + 1 - core})

    def conv_x(i, source):
        return remote(csend.at[1], crx.at[source], cv_x.at[0, i], cv_x.at[1, source],
                      {"outer": i * 2 + core})

    def conv_z(i, source):
        return remote(csend.at[2], crz.at[source], cv_z.at[0, i], cv_z.at[1, source], {"seq": i})

    weight(2, gp)
    stage_core(2)
    conv_core.start()

    def gin_tile(i, carry):
        rows = pl.ds(pl.multiple_of(i * TILE, TILE), TILE)
        total = mm(gq[rows, :], wq[...], NT)
        total = total + mm(gp[rows, :], wk[...], NT)
        total = total + mm(gv[rows, :], wv[...], NT)
        gin[rows, :] = total.astype(BF)
        return carry

    quarter = tiles // 4
    lax.fori_loop(0, quarter, gin_tile, 0)
    stage_x(2)
    stage_az(0)
    stage_z(1)
    lax.fori_loop(quarter, 2 * quarter, gin_tile, 0)
    conv_core.wait_recv()
    csend[1] = csend[0] + crc[...]
    others(X, x, lambda i: conv_x(i, x).start())
    stage_z(2)
    stage_ax(0)
    stage_az(1)
    lax.fori_loop(2 * quarter, tiles, gin_tile, 0)
    stage_az(2)
    stage_ac(0)
    stage_ax(1)
    others(X, x, lambda i: conv_x(i, i).wait_recv())
    crx[x] = csend[1]
    total = crx[0]
    for i in range(1, X):
        total = total + crx[i]
    csend[2] = total
    others(Z, z, lambda i: conv_z(i, z).start())
    stage_ax(2)
    stage_ac(1)
    stage_ac(2)
    others(Z, z, lambda i: conv_z(i, i).wait_recv())
    crz[z] = csend[2]
    total = crz[0]
    for i in range(1, Z):
        total = total + crz[i]
    conv_out[...] = total
    others(Z, z, lambda i: to_owner(i, z).wait_send())
    others(outer_count, o, lambda i: to_outer(i, o).wait_send())
    others(Z, z, lambda i: to_member(i, z).wait_send())
    conv_core.wait_send()
    others(X, x, lambda i: conv_x(i, x).wait_send())
    others(Z, z, lambda i: conv_z(i, z).wait_send())
    stage_end(0)
    stage_end(1)
    stage_end(2)


def on_device(seq_count, outer_count, inputs, grad_out, w_query, w_key, w_value, conv_taps):
    length = inputs.shape[0]
    Z, X = seq_count, outer_count // 2
    N = seq_count * outer_count
    r = D // N
    blocks = length // BLOCK
    vm = pltpu.VMEM
    dma = pltpu.SemaphoreType.DMA
    full = vm((length, D), BF)
    edge = vm((EDGE, D), BF)
    state = vm((blocks, PAIRS, HEAD_DIM, PAIR), F32)
    rows_z = PAIRS * HEAD_DIM // Z
    sliced = vm((Z, 2, rows_z, PAIR), BF)
    parts = vm((Z, 2, rows_z, PAIR), F32)
    total = vm((2, rows_z, PAIR), BF)
    totals = vm((outer_count, 2, rows_z, PAIR), BF)
    square = vm((blocks, PAIRS, PAIR, PAIR), BF)
    scratch = [
        vm((length + 8, D), F32), full, full, full, full, full, vm((D, length), BF),
        vm((length, D), F32), vm((length, D), F32), full, vm((length + 8, D), F32), full, full,
        edge, edge, edge, edge,
        state, state, sliced, sliced, parts, total, totals, sliced, sliced, square, square,
        vm((3, 2, X, Z, r, D), BF), vm((3, X, Z, r, D), BF), vm((3, X, Z, r, D), BF),
        vm((3, X, Z, r, D), BF), vm((3, Z, r, D), BF), vm((3, Z, r, D), BF),
        vm((3, TAPS, D), F32), vm((TAPS, D), F32), vm((X, TAPS, D), F32), vm((Z, TAPS, D), F32),
        dma((4,)), dma((Z,)), dma((Z,)), dma((outer_count,)), dma((outer_count,)), dma((Z,)), dma((Z,)),
        dma((2,)), dma((2, X)), dma((2, Z)),
        dma((3, 2)), dma((3, X)), dma((3, X)), dma((3, Z)), dma((3, Z)),
        dma((3, Z)), dma((3, Z)), dma((3, X)), dma((3, X)), dma((3, 2)),
    ]
    spec = pl.BlockSpec(memory_space=pltpu.VMEM)
    grad_inputs, weights, grad_conv = pl.pallas_call(
        functools.partial(kernel, seq_count, outer_count),
        out_shape=(
            jax.ShapeDtypeStruct((length, D), BF),
            jax.ShapeDtypeStruct((3, 2, X, Z, r, D), BF),
            jax.ShapeDtypeStruct((TAPS, D), F32),
        ),
        in_specs=[spec] * 6,
        out_specs=(spec, spec, spec),
        scratch_shapes=scratch,
        compiler_params=pltpu.CompilerParams(
            collective_id=0, has_side_effects=True, vmem_limit_bytes=56 * 1024 * 1024
        ),
    )(inputs, grad_out, w_query, w_key, w_value, conv_taps)
    weights = weights.reshape(3, D, D).astype(F32)
    return (grad_inputs, weights[1], weights[2], weights[0], grad_conv)


def solution(mesh):
    rows = P(("grp", "outer", "seq"), None)
    body = functools.partial(on_device, mesh.shape["seq"], mesh.shape["outer"])
    return jax.shard_map(
        body,
        mesh=mesh,
        in_specs=(rows, rows, P(), P(), P(), P()),
        out_specs=(rows, P("grp", None), P("grp", None), P("grp", None), P("grp", None)),
        check_vma=False,
    )
```
